128 devices in a mesh: group: 4 (over x_lo, core), tensor: 32 (over z, x_hi, y).
Axes of the slice: x: 4 (x_hi: 2, x_lo: 2; x = x_hi * 2 + x_lo), y: 4, z: 4, core: 2. Of those that a mesh axis runs over, the one named last changes fastest.
Arguments:
- hidden_in: bfloat16 [32768, 1536], P(('group', 'tensor')), may hold values from -6 to 6
- request_ids: int32 [128, 256], P(('group', 'tensor')), may hold values from 0 to 3, never falling along the last dimension, each value on 1 to 128 neighbouring positions
- norm_gains: float32 [2, 1536], replicated, may hold values from 0.5 to 1.5
- query_key_value_weight: bfloat16 [1536, 3072], replicated, may hold values from -0.15625 to 0.15625
- w_out: bfloat16 [1536, 1536], replicated, may hold values from -0.15625 to 0.15625
- w_in: bfloat16 [2, 1536, 4096], P(None, None, 'tensor'), may hold values from -0.15625 to 0.15625
- w_down: bfloat16 [4096, 1536], P('tensor'), may hold values from -0.09375 to 0.09375
- prefix_cache: bfloat16 [4, 1024, 1536], P('group', 'tensor'), may hold values from -210 to 210
- prefix_owner: int32 [32], replicated, may hold values from 0 to 3
- page_dest: int32 [2048, 1], P(('group', 'tensor')), may hold values from 0 to 3; in each aligned block of 16 rows (0 to 15, 16 to 31, ...) at most 8 rows name the same one
Outputs:
- hidden_out: bfloat16 [32768, 1536], P(('group', 'tensor'))
- suffix_cache: bfloat16 [4, 32, 4, 8, 16, 1536], P('group', 'tensor')
The draws below stay inside these ranges and needn't reach their ends.
Inputs may be any that keep to these rules, and one draw needn't show every extreme that they name: `request_ids`: each row numbers its requests from 0 in order of tokens, never falling, each request holding 1 to 128 tokens. `prefix_owner`: each block of the prefix cache is read from the slot of its owner only. `page_dest`: among the 16 pages of one device at most 8 have the same destination, and exactly 8 in some devices.
All inputs are finite; a program needn't handle non-finite values.
Results may differ from the reference program's by a relative error of at most 0.013.
The reference program's roundings to bfloat16 on the way count: a program that leaves them out, or rounds other values in their place, can miss the bound.
Values may be sent and summed in bfloat16 or wider, within the bound.
A program may use at most 192 MiB of HBM per device.

```python
import math
import jax
import jax.numpy as jnp
import numpy as np
from jax import lax

MODEL_DIMENSION = 1536
QUERY_HEADS = 16
KEY_VALUE_HEADS = 8
HEAD_DIMENSION = 96
FF = 4096
PREFIX_TOKENS = 1024
TOK_DEV = 256
PAGE = 16
REQ_DEV = 4
MOST = 128
PAGES_DEV = 16
CAP = 8
TOKENS = 32768
N_GROUP = 4
N_TENSOR = 32


def draw_prefix_cache(key, part):
    base_key = jax.random.fold_in(key, 0)
    cache_layout = (N_GROUP, PREFIX_TOKENS, 2 * KEY_VALUE_HEADS * HEAD_DIMENSION)
    drawn = jax.random.truncated_normal(base_key, -6.0, 6.0, cache_layout, jnp.float32)
    return drawn.astype(jnp.bfloat16)


def set_ends(array, own_key, least, top_value):
    extent = array.shape
    index_at = [jax.random.randint(jax.random.fold_in(own_key, axis), (), 0, extent[axis]) for axis in range(len(extent))]
    array = array.at[tuple(index_at)].set(least)
    longest = extent.index(max(extent))
    index_at[longest] = (index_at[longest] + 1) % extent[longest]
    return array.at[tuple(index_at)].set(top_value)


def steps_of(key, shape, cuts, least, top_value):
    gain = 1.0
    for axis_at, blocks in cuts:
        draws = jax.random.uniform(jax.random.fold_in(jax.random.fold_in(key, 6), axis_at), (blocks,), jnp.float32, least / len(cuts), top_value / len(cuts))
        gain = gain * jnp.repeat(jnp.exp(draws), shape[axis_at] // blocks).reshape((-1,) + (1,) * (len(shape) - 1 - axis_at))
    return gain


def profile(amount, total, limit, slope):
    portions = [(1 << 20) // math.isqrt(rank ** slope) + 1 for rank in range(2, amount + 1)]
    rest, given = total - limit - (amount - 1), [1] * (amount - 1)
    while rest > 0:
        candidates = [i for i in range(amount - 1) if given[i] < limit]
        pool, remaining = sum([portions[i] for i in candidates]), rest
        for i in candidates:
            extra = min(limit - given[i], max(1, remaining * portions[i] // pool), rest)
            given[i] = given[i] + extra
            rest = rest - extra
    return np.array([limit] + given)


def uneven_parts(rng, count, total, reach, slope):
    if count == 2:
        one = jax.random.randint(rng, (), max(1, total - reach), min(reach, total - 1) + 1)
        return jnp.stack([one, total - one])
    tallies = jnp.asarray(profile(count, total, reach, slope), jnp.int32)
    couples = (count - 1) // 2
    donor, taker = tallies[1:1 + 2 * couples:2], tallies[2:2 + 2 * couples:2]
    room = jnp.minimum(donor - 1, reach - taker)
    shifted = jax.random.randint(jax.random.fold_in(rng, 1), (couples,), 0, 1 << 20) % (room + 1)
    tallies = tallies.at[1:1 + 2 * couples:2].set(donor - shifted).at[2:2 + 2 * couples:2].set(taker + shifted)
    return tallies[jax.random.permutation(jax.random.fold_in(rng, 2), count)]


def routed_block(key, own, number, rows, amount, top, bound, skew):
    order = jax.random.permutation(key, amount)
    heavy_load, common = portions_of(amount, rows * top, bound, skew, True), portions_of(amount, rows * top, bound, skew, False)
    places = jnp.arange(amount)

    def named(sizes, rotation):
        used = int((sizes > 0).sum())
        fixed = max(1, used // 4)
        shifted = fixed + (places - fixed + rotation * (used - fixed)) % max(1, amount - fixed)
        return jnp.zeros((amount,), jnp.int32).at[order[jnp.where(places < fixed, places, shifted)]].set(jnp.asarray(sizes, jnp.int32))

    sizes = jnp.where(number % 4 == 0, named(heavy_load, number // 4), named(common, number - number // 4 - 1))
    mixed = jax.random.permutation(jax.random.fold_in(own, 3), amount)
    source_of, taker = mixed[0:amount // 2 * 2:2], mixed[1:amount // 2 * 2:2]
    margin = jnp.minimum(sizes[source_of] - 1, bound - sizes[taker]) // 2
    margin = jnp.where((source_of == order[0]) | (taker == order[0]) | (sizes[taker] == 0), 0, jnp.maximum(margin, 0))
    shifted = jax.random.randint(jax.random.fold_in(own, 4), (amount // 2,), 0, 1 << 20) % (margin + 1)
    sizes = sizes.at[source_of].add(-shifted).at[taker].add(shifted)
    items = jnp.searchsorted(jnp.cumsum(sizes), jnp.arange(rows * top), side="right").astype(jnp.int32)
    table = items.reshape(top, rows).T
    table = table[jax.random.permutation(jax.random.fold_in(own, 1), rows)]
    rotation = jax.random.randint(jax.random.fold_in(own, 2), (rows, 1), 0, top)
    return jnp.take_along_axis(table, (jnp.arange(top)[None, :] + rotation) % top, axis=1)


def portions_of(number_of, total, limit, skew, full):
    loads = [(1 << 20) // math.isqrt(standing ** skew) + 1 for standing in range(1, number_of + 1)]
    largest = limit if full else min(limit, max(-(-total // number_of), total * loads[0] // sum(loads)))
    least = 1 if total - largest >= number_of - 1 else 0
    given, spare = [largest] + [least] * (number_of - 1), total - largest - least * (number_of - 1)
    while spare > 0:
        candidates = [i for i in range(1, number_of) if given[i] < largest] or [i for i in range(1, number_of) if given[i] < limit]
        mass, budget = sum([loads[i] for i in candidates]), spare
        for i in candidates:
            addition = min(limit - given[i], max(1, budget * loads[i] // mass), spare)
            given[i] = given[i] + addition
            spare = spare - addition
    return np.array(given)


def noise(rng, extent, width, limit, cuts=(), kind=jnp.bfloat16):
    values = width * jax.random.normal(rng, extent, jnp.float32)
    if cuts:
        values = values * steps_of(rng, extent, cuts, -0.22, 0.18)
    return jnp.clip(values, -limit, limit).astype(kind)


def setup_inputs(seed: int = 0) -> dict:
    seeds = jax.random.split(jax.random.key(seed), 11)
    hidden_in = noise(seeds[0], (TOKENS, MODEL_DIMENSION), 1.0, 6.0, ((0, 128),))
    request_ids = jax.vmap(lambda own: jnp.searchsorted(jnp.cumsum(uneven_parts(own, REQ_DEV, TOK_DEV, MOST, 1)), jnp.arange(TOK_DEV), side="right"))(jax.random.split(seeds[1], (N_GROUP * N_TENSOR))).reshape((N_GROUP * N_TENSOR, TOK_DEV)).astype(jnp.int32)
    norm_gains = jnp.clip(1.0 + 0.1 * jax.random.normal(seeds[2], (2, MODEL_DIMENSION), jnp.float32), 0.5, 1.5)
    query_key_value_weight = noise(seeds[3], (MODEL_DIMENSION, (QUERY_HEADS + 2 * KEY_VALUE_HEADS) * HEAD_DIMENSION), MODEL_DIMENSION ** -0.5, 0.15625)
    w_out = noise(seeds[4], (QUERY_HEADS * HEAD_DIMENSION, MODEL_DIMENSION), (QUERY_HEADS * HEAD_DIMENSION) ** -0.5, 0.15625)
    w_in = noise(seeds[5], (2, MODEL_DIMENSION, FF), MODEL_DIMENSION ** -0.5, 0.15625, ((2, 32),))
    w_down = noise(seeds[6], (FF, MODEL_DIMENSION), FF ** -0.5, 0.09375, ((0, 32),))
    prefix_cache = draw_prefix_cache(jax.random.fold_in(seeds[10], 71), 0)
    prefix_owner = set_ends(jax.random.randint(seeds[8], (N_TENSOR,), 0, N_GROUP), jax.random.fold_in(seeds[8], 1), 0, N_GROUP - 1).astype(jnp.int32)
    page_dest_keys = jax.random.split(jax.random.fold_in(seeds[9], 1), (N_GROUP * N_TENSOR * PAGES_DEV) // PAGES_DEV)
    page_dest_turns = jax.random.permutation(jax.random.fold_in(seeds[9], 3), (N_GROUP * N_TENSOR * PAGES_DEV) // PAGES_DEV)
    page_dest = jax.vmap(lambda own, number: routed_block(jax.random.fold_in(seeds[9], 2), own, number, PAGES_DEV, N_GROUP, 1, CAP, 2))(page_dest_keys, page_dest_turns).reshape((N_GROUP * N_TENSOR * PAGES_DEV, 1))
    return {"hidden_in": hidden_in, "request_ids": request_ids, "norm_gains": norm_gains, "query_key_value_weight": query_key_value_weight, "w_out": w_out, "w_in": w_in, "w_down": w_down, "prefix_cache": prefix_cache, "prefix_owner": prefix_owner, "page_dest": page_dest}


ROPE_BASE = 100000.0
EPSILON = 1e-05
NEGATIVE_FILLER = -1e+30

def rms_norm(inputs, gain_row):
    floated = inputs.astype(jnp.float32)
    return floated * lax.rsqrt(lax.optimization_barrier(jnp.mean(floated * floated, axis=-1, keepdims=True)) + EPSILON) * gain_row

def apply_rotary(head_values, locate_position):
    half_dim = head_values.shape[-1] // 2
    frequency = ROPE_BASE ** (-jnp.arange(half_dim, dtype=jnp.float32) / half_dim)
    angles = locate_position.astype(jnp.float32)[:, None] * frequency[None, :]
    cosine = jnp.cos(angles)[:, None, :]
    sine_part = jnp.sin(angles)[:, None, :]
    first_half = head_values[..., :half_dim]
    second_half = head_values[..., half_dim:]
    return jnp.concatenate([first_half * cosine - second_half * sine_part, second_half * cosine + first_half * sine_part], axis=-1)

def positions(segment):
    row_number = segment.shape[0]
    row_index = jnp.arange(row_number, dtype=jnp.int32)
    same_request = segment[:, None] == segment[None, :]
    first_row = lax.optimization_barrier(jnp.min(jnp.where(same_request, row_index[None, :], row_number), axis=1)).astype(jnp.int32)
    return PREFIX_TOKENS + row_index - first_row

def layer_device(device_rows, segment, prefix_rows, norm_gains, query_key_value_weight, w_out, w_in, w_down):
    row_number = device_rows.shape[0]
    query_columns = QUERY_HEADS * HEAD_DIMENSION
    key_value_width = KEY_VALUE_HEADS * HEAD_DIMENSION
    normed = rms_norm(device_rows, norm_gains[0]).astype(jnp.bfloat16)
    projected_rows = jnp.dot(normed, query_key_value_weight, preferred_element_type=jnp.float32)
    locate_position = positions(segment)
    query_rows = apply_rotary(projected_rows[:, :query_columns].reshape(row_number, QUERY_HEADS, HEAD_DIMENSION), locate_position).astype(jnp.bfloat16)
    fresh_keys = apply_rotary(projected_rows[:, query_columns:query_columns + key_value_width].reshape(row_number, KEY_VALUE_HEADS, HEAD_DIMENSION), locate_position).astype(jnp.bfloat16)
    fresh_values = projected_rows[:, query_columns + key_value_width:].reshape(row_number, KEY_VALUE_HEADS, HEAD_DIMENSION).astype(jnp.bfloat16)
    joined_keys = jnp.concatenate([prefix_rows[:, :key_value_width].reshape(PREFIX_TOKENS, KEY_VALUE_HEADS, HEAD_DIMENSION), fresh_keys], axis=0)
    joined_values = jnp.concatenate([prefix_rows[:, key_value_width:].reshape(PREFIX_TOKENS, KEY_VALUE_HEADS, HEAD_DIMENSION), fresh_values], axis=0)
    query_groups = query_rows.reshape(row_number, KEY_VALUE_HEADS, QUERY_HEADS // KEY_VALUE_HEADS, HEAD_DIMENSION).astype(jnp.float32)
    scores = jnp.einsum('rkgd,nkd->rkgn', query_groups, joined_keys.astype(jnp.float32)) * HEAD_DIMENSION ** (-0.5)
    row_index = jnp.arange(row_number, dtype=jnp.int32)
    suffix_ok = (segment[None, :] == segment[:, None]) & (row_index[None, :] <= row_index[:, None])
    full_ok = jnp.concatenate([jnp.ones((row_number, PREFIX_TOKENS), dtype=bool), suffix_ok], axis=1)
    scores = jnp.where(full_ok[:, None, None, :], scores, NEGATIVE_FILLER)
    row_max = lax.optimization_barrier(jnp.max(scores, axis=-1, keepdims=True))
    weights = jnp.exp(scores - row_max)
    totals = lax.optimization_barrier(jnp.sum(weights, axis=-1))
    rounded = lax.optimization_barrier(weights.astype(jnp.bfloat16))
    summed = jnp.einsum('rkgn,nkd->rkgd', rounded.astype(jnp.float32), joined_values.astype(jnp.float32))
    attended = (summed / totals[..., None]).reshape(row_number, QUERY_HEADS * HEAD_DIMENSION).astype(jnp.bfloat16)
    middle = (device_rows.astype(jnp.float32) + jnp.dot(attended, w_out, preferred_element_type=jnp.float32)).astype(jnp.bfloat16)
    second = rms_norm(middle, norm_gains[1]).astype(jnp.bfloat16)
    gate_proj = jnp.dot(second, w_in[0], preferred_element_type=jnp.float32)
    up_proj = jnp.dot(second, w_in[1], preferred_element_type=jnp.float32)
    activated = (jax.nn.silu(gate_proj) * up_proj).astype(jnp.bfloat16)
    hidden_out = (middle.astype(jnp.float32) + jnp.dot(activated, w_down, preferred_element_type=jnp.float32)).astype(jnp.bfloat16)
    cache_rows = jnp.concatenate([fresh_keys.reshape(row_number, key_value_width), fresh_values.reshape(row_number, key_value_width)], axis=1)
    return (hidden_out, cache_rows)

def reference(hidden_in, request_ids, norm_gains, query_key_value_weight, w_out, w_in, w_down, prefix_cache, prefix_owner, page_dest):
    device_total = N_GROUP * N_TENSOR
    cache_columns = 2 * KEY_VALUE_HEADS * HEAD_DIMENSION
    blocked = prefix_cache.reshape(N_GROUP, N_TENSOR, PREFIX_TOKENS // N_TENSOR, cache_columns)
    prefix_rows = blocked[prefix_owner, jnp.arange(N_TENSOR, dtype=jnp.int32)].reshape(PREFIX_TOKENS, cache_columns)
    device_rows = hidden_in.reshape(device_total, TOK_DEV, MODEL_DIMENSION)

    def per_device(operand):
        return layer_device(operand[0], operand[1], prefix_rows, norm_gains, query_key_value_weight, w_out, w_in, w_down)
    outputs, caches = lax.map(per_device, (device_rows, request_ids))
    hidden_out = outputs.reshape(TOKENS, MODEL_DIMENSION)
    page_blocks = caches.reshape(N_GROUP, N_TENSOR, PAGES_DEV, PAGE * cache_columns).astype(jnp.float32)
    destination = page_dest.reshape(N_GROUP, N_TENSOR, PAGES_DEV)
    group_iota = jnp.arange(N_GROUP, dtype=jnp.int32)
    onehot = (destination[..., None] == group_iota).astype(jnp.int32)
    page_rank = lax.optimization_barrier(jnp.sum((jnp.cumsum(onehot, axis=2) - onehot) * onehot, axis=3))
    slot_iota = jnp.arange(CAP, dtype=jnp.int32)
    select = ((destination[..., None, None] == group_iota[:, None]) & (page_rank[..., None, None] == slot_iota[None, :])).astype(jnp.float32)
    placed = jnp.einsum('gtpdj,gtpc->dtgjc', select, page_blocks)
    suffix_cache = placed.reshape(N_GROUP, N_TENSOR, N_GROUP, CAP, PAGE, cache_columns).astype(jnp.bfloat16)
    return (hidden_out, suffix_cache)
```

```python
import functools

import jax
import jax.numpy as jnp
from jax import lax
from jax.experimental import pallas as pl
from jax.experimental.pallas import tpu as pltpu
from jax.sharding import PartitionSpec as P

QUERY_HEADS = 16
KEY_VALUE_HEADS = 8
HEAD_DIMENSION = 96
PREFIX_TOKENS = 1024
CAP = 8
WIDTH = 1536
HALF = 768
MESH = pl.DeviceIdType.MESH


ROPE_BASE = 100000.0
EPSILON = 1e-05
NEGATIVE_FILLER = -1e30


N_Z, N_H, N_Y = 4, 2, 4
DIRECTIONS = ("x", "y+", "y-", "z+", "z-", "sib")
ALL = slice(None)


class Plan:
    def __init__(self):
        self.copies = []

    def add(self, buffer, source, target, direction, after, size):
        self.copies.append((buffer, source, target, direction, tuple(after), size))
        return len(self.copies) - 1

    def ring(self, buffer, axis, after, block, size):
        up = self.add(buffer, block(0, None), block(3, None), axis + "+", after, size)
        down = self.add(buffer, block(0, None), block(1, None), axis + "-", after, size)
        far_up = self.add(buffer, block(3, 0), block(2, 0), axis + "+", [up], size / 2)
        far_down = self.add(buffer, block(1, 1), block(2, 1), axis + "-", [down], size / 2)
        return [up, down, far_up, far_down]

    def piece(self, buffer, order, cut, size, after=()):
        index = lambda z, h, y, part: (z, h, y) + cut(part)
        done = []
        if order[0] == "x":
            swap = self.add(buffer, index(0, 0, 0, None), index(0, 1, 0, None), "x", after, size)
            done.append(swap)
            for h, first in ((0, list(after)), (1, [swap])):
                if order[1] == "y":
                    near = self.ring(buffer, "y", first, lambda d, p, h=h: index(0, h, d, p), size)
                    far = self.ring(buffer, "z", near, lambda d, p, h=h: index(d, h, ALL, p), 4 * size)
                else:
                    near = self.ring(buffer, "z", first, lambda d, p, h=h: index(d, h, 0, p), size)
                    far = self.ring(buffer, "y", near, lambda d, p, h=h: index(ALL, h, d, p), 4 * size)
                done += near + far
        else:
            if order[0] == "y":
                near = self.ring(buffer, "y", list(after), lambda d, p: index(0, 0, d, p), size)
                far = self.ring(buffer, "z", near, lambda d, p: index(d, 0, ALL, p), 4 * size)
                at = lambda d, h: index(d, h, ALL, None)
            else:
                near = self.ring(buffer, "z", list(after), lambda d, p: index(d, 0, 0, p), size)
                far = self.ring(buffer, "y", near, lambda d, p: index(ALL, 0, d, p), 4 * size)
                at = lambda d, h: index(ALL, h, d, None)
            done += near + far
            for d, need in ((0, near), (3, far[:1]), (1, far[1:2]), (2, far[2:])):
                done.append(self.add(buffer, at(d, 0), at(d, 1), "x", need, 4 * size))
        return done

    def order(self, link=46.0, chip=250.0, latency=1600.0):
        free = {d: 0.0 for d in DIRECTIONS}
        arrival, issued, left, now = {}, [], list(range(len(self.copies))), 0.0
        while left:
            ready = {k: max([now] + [arrival[d] for d in self.copies[k][4]]) for k in left
                     if all(d in arrival for d in self.copies[k][4])}
            pick = min(ready, key=lambda k: (ready[k], k))
            now = ready[pick]
            direction, size = self.copies[pick][3], self.copies[pick][5]
            start = max(now, free[direction])
            free[direction] = start + size / (chip if direction == "sib" else link)
            arrival[pick] = free[direction] + latency
            issued.append(pick)
            left.remove(pick)
        return issued, arrival


def gather_plan():
    plan = Plan()

    def prefix_cut(first):
        return lambda part: (
            pl.ds(first, 16),
            pl.ds(0, HALF) if part is None else pl.ds(384 * part, 384),
        )

    def row_cut(first, count):
        return lambda part: (
            pl.ds(first, count) if part is None else pl.ds(first + count // 2 * part, count // 2),
            ALL,
        )

    done = plan.piece("prefix", "xyz", prefix_cut(0), 16 * HALF * 2)
    done += plan.piece("prefix", "xzy", prefix_cut(16), 16 * HALF * 2)
    plan.add("prefix", (), (), "sib", done, 32 * 32 * HALF * 2)
    plan.piece("in", "xyz", row_cut(0, HALF), HALF * 256)
    plan.piece("in", "xzy", row_cut(HALF, HALF), HALF * 256)
    plan.piece("down", "yzx", row_cut(0, 32), 32 * WIDTH * 2)
    plan.piece("down", "zyx", row_cut(32, 32), 32 * WIDTH * 2)
    return plan


def neighbours():
    g, t = lax.axis_index("group"), lax.axis_index("tensor")
    core, low = g % 2, g // 2
    y, high, z = t % 4, (t // 4) % 2, t // 8

    def at(zz, hh, yy):
        return (zz % 4) * 8 + hh * 4 + yy % 4

    return {
        "x": ((1 - low) * 2 + core, at(z, 1 - high, y)),
        "y+": (g, at(z, high, y + 1)),
        "y-": (g, at(z, high, y + 3)),
        "z+": (g, at(z + 1, high, y)),
        "z-": (g, at(z + 3, high, y)),
        "sib": (low * 2 + 1 - core, t),
        "twin": ((1 - low) * 2 + core, t),
        "cross": ((1 - low) * 2 + 1 - core, t),
    }


def gather_kernel(
    owned, block, win, wdown, pages_ref, win_ref, wdown_ref, rival, chosen, local, cand_send, cand_recv, send, recv
):
    core = lax.axis_index("group") % 2
    near = neighbours()
    barrier = pltpu.get_barrier_semaphore()
    for target in near.values():
        pl.semaphore_signal(barrier, inc=1, device_id=target, device_id_type=MESH)
    pl.semaphore_wait(barrier, len(near))

    plan = gather_plan()
    own = [
        pltpu.make_async_copy(win, win_ref.at[0, 0, 0], local.at[0]),
        pltpu.make_async_copy(wdown, wdown_ref.at[0, 0, 0], local.at[1]),
    ]
    rivals = [
        pltpu.make_async_remote_copy(
            src_ref=block.at[half],
            dst_ref=rival.at[slot],
            send_sem=cand_send.at[slot],
            recv_sem=cand_recv.at[slot],
            device_id=near[name],
            device_id_type=MESH,
        )
        for slot, (name, half) in enumerate((("sib", 1 - core), ("twin", core), ("cross", 1 - core)))
    ]
    for copy in rivals + own:
        copy.start()
    total = jnp.where(owned[0] > 0.5, block[core], jnp.zeros_like(block[core]))
    for slot, copy in enumerate(rivals):
        copy.wait_recv()
        total = jnp.where(owned[slot + 1] > 0.5, rival[slot], total)
    chosen[...] = total
    last = pltpu.make_async_copy(chosen, pages_ref.at[core, 0, 0, 0], local.at[2])
    last.start()
    for copy in own + [last]:
        copy.wait()

    def place(name, index):
        if name == "prefix":
            return pages_ref.at[core].at[index] if index else pages_ref.at[core]
        return {"in": win_ref, "down": wdown_ref}[name].at[index]

    order, _ = plan.order()
    copies, arrived = {}, set()
    for k in order:
        name, source, target, direction, after, _ = plan.copies[k]
        for other in after:
            if other not in arrived:
                copies[other].wait_recv()
                arrived.add(other)
        copies[k] = pltpu.make_async_remote_copy(
            src_ref=place(name, source),
            dst_ref=place(name, target),
            send_sem=send.at[k],
            recv_sem=recv.at[k],
            device_id=near[direction],
            device_id_type=MESH,
        )
        copies[k].start()
    for k in order:
        if k not in arrived:
            copies[k].wait_recv()
    for k in order:
        copies[k].wait_send()
    for copy in rivals:
        copy.wait_send()


def gather(owned, block, win, wdown):
    count = len(gather_plan().copies)
    vmem = pl.BlockSpec(memory_space=pltpu.VMEM)
    return pl.pallas_call(
        gather_kernel,
        out_shape=(
            jax.ShapeDtypeStruct((2, 4, 2, 4, 32, HALF), jnp.bfloat16),
            jax.ShapeDtypeStruct((4, 2, 4, WIDTH, 128), jnp.bfloat16),
            jax.ShapeDtypeStruct((4, 2, 4, 64, WIDTH), jnp.bfloat16),
        ),
        in_specs=[vmem] * 4,
        out_specs=(pl.BlockSpec(memory_space=pl.ANY),) * 3,
        scratch_shapes=[
            pltpu.VMEM((3, 32, HALF), jnp.bfloat16),
            pltpu.VMEM((32, HALF), jnp.bfloat16),
            pltpu.SemaphoreType.DMA((3,)),
            pltpu.SemaphoreType.DMA((3,)),
            pltpu.SemaphoreType.DMA((3,)),
            pltpu.SemaphoreType.DMA((count,)),
            pltpu.SemaphoreType.DMA((count,)),
        ],
        compiler_params=pltpu.CompilerParams(collective_id=0, has_side_effects=True),
    )(owned, block, win, wdown)


def rms_norm(inputs, gain_row):
    floated = inputs.astype(jnp.float32)
    return (
        floated
        * lax.rsqrt(jnp.mean(floated * floated, axis=-1, keepdims=True) + EPSILON)
        * gain_row
    )


def apply_rotary(head_values, locate_position):
    half_dim = head_values.shape[-1] // 2
    frequency = ROPE_BASE ** (-jnp.arange(half_dim, dtype=jnp.float32) / half_dim)
    angles = locate_position.astype(jnp.float32)[:, None] * frequency[None, :]
    cosine = jnp.cos(angles)[:, None, :]
    sine_part = jnp.sin(angles)[:, None, :]
    first_half = head_values[..., :half_dim]
    second_half = head_values[..., half_dim:]
    return jnp.concatenate(
        [
            first_half * cosine - second_half * sine_part,
            second_half * cosine + first_half * sine_part,
        ],
        axis=-1,
    )


def positions(segment):
    row_number = segment.shape[0]
    row_index = jnp.arange(row_number, dtype=jnp.int32)
    same_request = segment[:, None] == segment[None, :]
    first_row = jnp.min(jnp.where(same_request, row_index[None, :], row_number), axis=1)
    return PREFIX_TOKENS + row_index - first_row


def attend_update(attn_state, scores, value_head_rows):
    row_max, row_total, weighted = attn_state
    new_max = jnp.maximum(row_max, jnp.max(scores, axis=-1))
    weights = jnp.exp(scores - new_max[..., None])
    row_total = jnp.sum(weights, axis=-1)
    weighted = jnp.einsum(
        "rkgn,nkd->rkgd",
        weights.astype(jnp.bfloat16),
        value_head_rows,
        preferred_element_type=jnp.float32,
    )
    return (new_max, row_total, weighted)


def combine_states(left_state, right_state):
    new_max = jnp.maximum(left_state[0], right_state[0])
    left_factor = jnp.exp(left_state[0] - new_max)
    right_factor = jnp.exp(right_state[0] - new_max)
    row_total = left_state[1] * left_factor + right_state[1] * right_factor
    weighted = left_state[2] * left_factor[..., None] + right_state[2] * right_factor[..., None]
    return (new_max, row_total, weighted)


def sibling_swap(array):
    pairs = [(0, 1), (1, 0), (2, 3), (3, 2)]
    return lax.ppermute(array, "group", pairs)


def on_device(
    hidden_in,
    request_ids,
    norm_gains,
    query_key_value_weight,
    w_out,
    w_in,
    w_down,
    prefix_cache,
    prefix_owner,
    page_dest,
):
    token_rows = hidden_in.shape[0]
    query_columns = QUERY_HEADS * HEAD_DIMENSION
    key_value_width = KEY_VALUE_HEADS * HEAD_DIMENSION
    me = lax.axis_index("group")
    core = me % 2
    owner_row = prefix_owner[lax.axis_index("tensor")]
    owned = jnp.broadcast_to(
        (owner_row == jnp.bitwise_xor(me, jnp.arange(4, dtype=jnp.int32)))[:, None, None], (4, 1, HALF)
    ).astype(jnp.float32)
    win = lax.dynamic_slice_in_dim(w_in, 64 * core, 64, axis=2)
    win = jnp.concatenate([win[0], win[1]], axis=1)
    wdown = lax.dynamic_slice_in_dim(w_down, 64 * core, 64, axis=0)
    block = jnp.stack([prefix_cache[0][:, :HALF], prefix_cache[0][:, HALF:]])
    pages, win, wdown = gather(owned, block, win, wdown)

    segment = request_ids[0]
    normed = rms_norm(hidden_in, norm_gains[0]).astype(jnp.bfloat16)
    projected_rows = jnp.dot(normed, query_key_value_weight, preferred_element_type=jnp.float32)
    locate_position = positions(segment)
    query_rows = apply_rotary(
        projected_rows[:, :query_columns].reshape(token_rows, QUERY_HEADS, HEAD_DIMENSION),
        locate_position,
    ).astype(jnp.bfloat16)
    fresh_keys = apply_rotary(
        projected_rows[:, query_columns : query_columns + key_value_width].reshape(
            token_rows, KEY_VALUE_HEADS, HEAD_DIMENSION
        ),
        locate_position,
    ).astype(jnp.bfloat16)
    fresh_values = (
        projected_rows[:, query_columns + key_value_width :]
        .reshape(token_rows, KEY_VALUE_HEADS, HEAD_DIMENSION)
        .astype(jnp.bfloat16)
    )
    query_groups = query_rows.reshape(
        token_rows, KEY_VALUE_HEADS, QUERY_HEADS // KEY_VALUE_HEADS, HEAD_DIMENSION
    )
    score_scale = HEAD_DIMENSION ** (-0.5)
    row_index = jnp.arange(token_rows, dtype=jnp.int32)
    allowed = (segment[None, :] == segment[:, None]) & (row_index[None, :] <= row_index[:, None])
    local_scores = (
        jnp.einsum("rkgd,nkd->rkgn", query_groups, fresh_keys, preferred_element_type=jnp.float32)
        * score_scale
    )
    local_scores = jnp.where(allowed[:, None, None, :], local_scores, NEGATIVE_FILLER)
    empty_state = (
        jnp.full(
            (token_rows, KEY_VALUE_HEADS, QUERY_HEADS // KEY_VALUE_HEADS),
            NEGATIVE_FILLER,
            jnp.float32,
        ),
        None,
        None,
    )
    local_state = attend_update(empty_state, local_scores, fresh_values)
    key_head_rows = pages[0].reshape(PREFIX_TOKENS, KEY_VALUE_HEADS, HEAD_DIMENSION)
    value_head_rows = pages[1].reshape(PREFIX_TOKENS, KEY_VALUE_HEADS, HEAD_DIMENSION)
    scores = (
        jnp.einsum(
            "rkgd,nkd->rkgn", query_groups, key_head_rows, preferred_element_type=jnp.float32
        )
        * score_scale
    )
    attn_state = attend_update(empty_state, scores, value_head_rows)
    attn_state = combine_states(attn_state, local_state)
    attended = (
        (attn_state[2] / attn_state[1][..., None])
        .reshape(token_rows, QUERY_HEADS * HEAD_DIMENSION)
        .astype(jnp.bfloat16)
    )
    middle = (
        hidden_in.astype(jnp.float32) + jnp.dot(attended, w_out, preferred_element_type=jnp.float32)
    ).astype(jnp.bfloat16)
    second = rms_norm(middle, norm_gains[1]).astype(jnp.bfloat16)
    both = jnp.concatenate([second, sibling_swap(second)], axis=0)
    win = win.reshape(32, WIDTH, 128)
    product = jnp.einsum("mk,skn->smn", both, win, preferred_element_type=jnp.float32)
    activated = (jax.nn.silu(product[..., :64]) * product[..., 64:]).astype(jnp.bfloat16)
    partial = jnp.einsum(
        "smn,snd->md", activated, wdown.reshape(32, 64, WIDTH), preferred_element_type=jnp.float32
    )
    mlp_out = partial[:token_rows] + sibling_swap(partial[token_rows:])
    hidden_out = (middle.astype(jnp.float32) + mlp_out).astype(jnp.bfloat16)
    cache_rows = jnp.concatenate(
        [
            fresh_keys.reshape(token_rows, key_value_width),
            fresh_values.reshape(token_rows, key_value_width),
        ],
        axis=1,
    )
    page_count = page_dest.shape[0]
    page_blocks = cache_rows.reshape(page_count, token_rows // page_count, 2 * key_value_width)
    destination = page_dest[:, 0]
    dest_count = lax.axis_size("group")
    group_iota = jnp.arange(dest_count, dtype=jnp.int32)
    onehot = (destination[:, None] == group_iota[None, :]).astype(jnp.int32)
    page_rank = jnp.sum((jnp.cumsum(onehot, axis=0) - onehot) * onehot, axis=1)
    slot_iota = jnp.arange(CAP, dtype=jnp.int32)
    select = (
        (destination[:, None, None] == group_iota[None, :, None])
        & (page_rank[:, None, None] == slot_iota[None, None, :])
    ).astype(jnp.bfloat16)
    outgoing = jnp.einsum(
        "pdj,pxc->djxc", select, page_blocks, preferred_element_type=jnp.float32
    ).astype(jnp.bfloat16)
    received = lax.all_to_all(outgoing, "group", split_axis=0, concat_axis=0, tiled=True)
    return (hidden_out, received[None, None])


def solution(mesh):
    return jax.shard_map(
        on_device,
        mesh=mesh,
        in_specs=(
            P(("group", "tensor"), None),
            P(("group", "tensor"), None),
            P(),
            P(),
            P(),
            P(None, None, "tensor"),
            P("tensor", None),
            P("group", "tensor", None),
            P(),
            P(("group", "tensor"), None),
        ),
        out_specs=(P(("group", "tensor"), None), P("group", "tensor", None, None, None, None)),
        check_vma=False,
    )
```

```python
import functools

import jax
import jax.numpy as jnp
import numpy as np
from jax import lax
from jax.experimental import pallas as pl
from jax.experimental.pallas import tpu as pltpu
from jax.sharding import PartitionSpec as P

QUERY_HEADS = 16
KEY_VALUE_HEADS = 8
HEAD_DIMENSION = 96
PREFIX_TOKENS = 1024
CAP = 8
TOKENS = 256
PAGE = 16
WIDTH = 1536
HALF = 768
ROPE_BASE = 100000.0
EPSILON = 1e-05
NEGATIVE_FILLER = -1e30
MESH = pl.DeviceIdType.MESH
F32, BF16 = jnp.float32, jnp.bfloat16


N_Z, N_H, N_Y = 4, 2, 4
DIRECTIONS = ("x", "y+", "y-", "z+", "z-", "sib")
ALL = slice(None)


class Plan:
    def __init__(self):
        self.copies = []

    def add(self, buffer, source, target, direction, after, size):
        self.copies.append((buffer, source, target, direction, tuple(after), size))
        return len(self.copies) - 1

    def ring(self, buffer, axis, after, block, size):
        up = self.add(buffer, block(0, None), block(3, None), axis + "+", after, size)
        down = self.add(buffer, block(0, None), block(1, None), axis + "-", after, size)
        far_up = self.add(buffer, block(3, 0), block(2, 0), axis + "+", [up], size / 2)
        far_down = self.add(buffer, block(1, 1), block(2, 1), axis + "-", [down], size / 2)
        return [up, down, far_up, far_down]

    def piece(self, buffer, order, cut, size, after=()):
        index = lambda z, h, y, part: (z, h, y) + cut(part)
        done = []
        if order[0] == "x":
            swap = self.add(buffer, index(0, 0, 0, None), index(0, 1, 0, None), "x", after, size)
            done.append(swap)
            for h, first in ((0, list(after)), (1, [swap])):
                if order[1] == "y":
                    near = self.ring(buffer, "y", first, lambda d, p, h=h: index(0, h, d, p), size)
                    far = self.ring(buffer, "z", near, lambda d, p, h=h: index(d, h, ALL, p), 4 * size)
                else:
                    near = self.ring(buffer, "z", first, lambda d, p, h=h: index(d, h, 0, p), size)
                    far = self.ring(buffer, "y", near, lambda d, p, h=h: index(ALL, h, d, p), 4 * size)
                done += near + far
        else:
            if order[0] == "y":
                near = self.ring(buffer, "y", list(after), lambda d, p: index(0, 0, d, p), size)
                far = self.ring(buffer, "z", near, lambda d, p: index(d, 0, ALL, p), 4 * size)
                at = lambda d, h: index(d, h, ALL, None)
            else:
                near = self.ring(buffer, "z", list(after), lambda d, p: index(d, 0, 0, p), size)
                far = self.ring(buffer, "y", near, lambda d, p: index(ALL, 0, d, p), 4 * size)
                at = lambda d, h: index(ALL, h, d, None)
            done += near + far
            for d, need in ((0, near), (3, far[:1]), (1, far[1:2]), (2, far[2:])):
                done.append(self.add(buffer, at(d, 0), at(d, 1), "x", need, 4 * size))
        return done

    def order(self, work=(), link=46.0, chip=250.0, latency=1600.0):
        free = {d: 0.0 for d in DIRECTIONS}
        arrival, issued, now = {}, [], 0.0
        left, work = list(range(len(self.copies))), list(work)

        def known(needs):
            return all(d in arrival for d in needs)

        while left or work:
            ready = {k: max([0.0] + [arrival[d] for d in self.copies[k][4]]) for k in left if known(self.copies[k][4])}
            pick = min(ready, key=lambda k: (max(ready[k], now), k)) if ready else None
            if pick is not None and ready[pick] <= now:
                direction, size = self.copies[pick][3], self.copies[pick][5]
                free[direction] = max(now, free[direction]) + size / (chip if direction == "sib" else link)
                arrival[pick] = free[direction] + latency
                issued.append(("copy", pick))
                left.remove(pick)
                continue
            start = max([0.0] + [arrival[d] for d in work[0][2]]) if work and known(work[0][2]) else None
            if start is not None and (pick is None or start <= max(now, ready[pick])):
                now = max(now, start) + work[0][1]
                issued.append(("work", work.pop(0)))
                continue
            now = ready[pick]
        return issued, arrival, now


def gather_plan():
    plan = Plan()

    def prefix_cut(first):
        return lambda part: (
            pl.ds(first, 16),
            pl.ds(0, HALF) if part is None else pl.ds(384 * part, 384),
        )

    def row_cut(first, count):
        return lambda part: (
            pl.ds(first, count) if part is None else pl.ds(first + count // 2 * part, count // 2),
            ALL,
        )

    done = plan.piece("prefix", "xyz", prefix_cut(0), 16 * HALF * 2)
    done += plan.piece("prefix", "xzy", prefix_cut(16), 16 * HALF * 2)
    share = plan.add("prefix", (), (), "sib", done, 32 * 32 * HALF * 2)
    plan.piece("in", "xyz", row_cut(0, HALF), HALF * 256)
    plan.piece("in", "xzy", row_cut(HALF, HALF), HALF * 256)
    plan.piece("down", "yzx", row_cut(0, 32), 32 * WIDTH * 2)
    plan.piece("down", "zyx", row_cut(32, 32), 32 * WIDTH * 2)
    return plan, [share] + done


def covers(plan, z, high):
    fits = lambda index, at: index == ALL or index == at
    return [
        k
        for k, (name, _, target, _, _, _) in enumerate(plan.copies)
        if name != "prefix" and fits(target[0], z) and fits(target[1], high)
    ]


def neighbours():
    g, t = lax.axis_index("group"), lax.axis_index("tensor")
    core, low = g % 2, g // 2
    y, high, z = t % 4, (t // 4) % 2, t // 8

    def at(zz, hh, yy):
        return (zz % 4) * 8 + hh * 4 + yy % 4

    return {
        "x": ((1 - low) * 2 + core, at(z, 1 - high, y)),
        "y+": (g, at(z, high, y + 1)),
        "y-": (g, at(z, high, y + 3)),
        "z+": (g, at(z + 1, high, y)),
        "z-": (g, at(z + 3, high, y)),
        "sib": (low * 2 + 1 - core, t),
        "twin": ((1 - low) * 2 + core, t),
        "cross": ((1 - low) * 2 + 1 - core, t),
    }


def rope_table():
    half = HEAD_DIMENSION // 2
    frequency = (ROPE_BASE ** (-np.arange(half, dtype=np.float32) / half)).astype(np.float32)
    angles = (PREFIX_TOKENS + np.arange(128, dtype=np.float32))[None, :] * frequency[:, None]
    rest = np.concatenate([np.cos(angles.astype(np.float64)), np.sin(angles.astype(np.float64))]).astype(np.float32)
    parts = []
    for _ in range(3):
        parts.append(rest.astype(jnp.bfloat16))
        rest = rest - parts[-1].astype(np.float32)
    return np.concatenate(parts)


def norm_rows(values, gain):
    return values * lax.rsqrt(jnp.mean(values * values, axis=-1, keepdims=True) + EPSILON) * gain


def dot(left, right):
    return jnp.dot(left, right, preferred_element_type=F32)


def layer_kernel(
    hidden, segment_ref, gains, owner_ref, dest_ref, table, qkv_hbm, out_hbm, in_hbm, down_hbm, prefix_hbm,
    result, suffix,
    raw, block, rival, win, wdown, pages, qkv, w_out, cache, heads, mixed, turn, mask, outgoing, tokens, middle,
    normed, total, sent, received,
    local, cand_send, cand_recv, send, recv, swap_send, swap_recv, page_send, page_recv,
):
    group = lax.axis_index("group")
    core = group % 2
    near = neighbours()
    plan, prefix_done = gather_plan()

    def fetch(source, target, slot):
        copy = pltpu.make_async_copy(source, target, local.at[slot])
        copy.start()
        return copy

    columns = lambda at: pl.ds(pl.multiple_of(at * HALF, 128), HALF)
    first = [fetch(prefix_hbm.at[0, :, pl.ds(HALF * n, HALF)], block.at[n], n) for n in range(2)]
    weights = [fetch(in_hbm, raw, 2)]
    own = [fetch(down_hbm.at[pl.ds(pl.multiple_of(64 * core, 64), 64), :], wdown.at[0, 0, 0], 3)]
    loads = [fetch(qkv_hbm.at[:, pl.ds(384 * n, 384)], qkv.at[n], 4 + n) for n in range(8)]
    out_load = fetch(out_hbm, w_out, 12)

    barrier = pltpu.get_barrier_semaphore()
    for target in near.values():
        pl.semaphore_signal(barrier, inc=1, device_id=target, device_id_type=MESH)
    for copy in first:
        copy.wait()
    pl.semaphore_wait(barrier, len(near))

    rivals = [
        pltpu.make_async_remote_copy(
            src_ref=block.at[half],
            dst_ref=rival.at[slot],
            send_sem=cand_send.at[slot],
            recv_sem=cand_recv.at[slot],
            device_id=near[name],
            device_id_type=MESH,
        )
        for slot, (name, half) in enumerate((("sib", 1 - core), ("twin", core), ("cross", 1 - core)))
    ]
    for copy in rivals:
        copy.start()

    weights[0].wait()
    gate, up = raw[0].astype(F32), raw[1].astype(F32)
    low_lane = lax.broadcasted_iota(jnp.int32, (WIDTH, 128), 1) < 64
    left = jnp.where(core == 0, gate, pltpu.roll(gate, 64, 1))
    right = jnp.where(core == 0, pltpu.roll(up, 64, 1), up)
    win[0, 0, 0] = jnp.where(low_lane, left, right).astype(BF16)

    tensor = lax.axis_index("tensor")
    owners = owner_ref[...]
    lanes = lax.broadcasted_iota(jnp.int32, owners.shape, 1)
    owner = jnp.sum(jnp.where(lanes == tensor, owners, 0), axis=1, keepdims=True)
    low = group // 2
    names = (group, low * 2 + 1 - core, (1 - low) * 2 + core, (1 - low) * 2 + 1 - core)
    chosen = jnp.where(owner == names[0], block[core], jnp.zeros((32, HALF), BF16))
    for slot, copy in enumerate(rivals):
        copy.wait_recv()
        chosen = jnp.where(owner == names[slot + 1], rival[slot], chosen)
    pages[core, 0, 0, 0] = chosen
    own[0].wait()

    def place(name, index):
        if name == "prefix":
            return pages.at[core].at[index] if index else pages.at[core]
        return {"in": win, "down": wdown}[name].at[index]

    def swap(source, target, slot, name, sems, arrivals):
        return pltpu.make_async_remote_copy(
            src_ref=source, dst_ref=target, send_sem=sems.at[slot], recv_sem=arrivals.at[slot],
            device_id=near[name], device_id_type=MESH,
        )

    swaps, page_copies, page_own = [], [], []

    def prepare():
        values = hidden[...].astype(F32)
        normed[...] = norm_rows(values, gains[0:1]).astype(BF16)
        segment = segment_ref[...].astype(F32)
        across = jnp.broadcast_to(segment, (TOKENS, TOKENS))
        key = lax.broadcasted_iota(jnp.int32, (TOKENS, TOKENS), 0)
        query = lax.broadcasted_iota(jnp.int32, (TOKENS, TOKENS), 1)
        allowed = jnp.where((across.T == across) & (key <= query), 1.0, 0.0)
        mask[...] = allowed
        offset = (jnp.sum(allowed, axis=0, keepdims=True) - 1.0).astype(jnp.int32)
        spot = lax.broadcasted_iota(jnp.int32, (128, TOKENS), 0) == offset
        parts = dot(table[...], jnp.where(spot, 1.0, 0.0).astype(BF16))
        turn[...] = parts[0:96] + parts[96:192] + parts[192:288]

    def rotate(rows):
        cosine, sine = turn[0:48], turn[48:96]
        out = []
        for n in range(4):
            one, two = rows[96 * n : 96 * n + 48], rows[96 * n + 48 : 96 * n + 96]
            out += [one * cosine - two * sine, two * cosine + one * sine]
        return out

    def project(n):
        loads[n].wait()
        projected = dot(normed[...], qkv[n])
        if n < 4:
            turned = rotate(projected.T)
            for m in range(4):
                heads[4 * n + m] = jnp.concatenate(turned[2 * m : 2 * m + 2], axis=0).astype(BF16)
        elif n < 6:
            cache[:, 384 * (n - 4) : 384 * (n - 3)] = jnp.concatenate(rotate(projected.T), axis=0).T.astype(BF16)
        else:
            cache[:, 384 * (n - 4) : 384 * (n - 3)] = projected.astype(BF16)

    def send_pages():
        page = lax.broadcasted_iota(jnp.int32, (PAGE, TOKENS), 0)
        token = lax.broadcasted_iota(jnp.int32, (PAGE, TOKENS), 1)
        dest = jnp.broadcast_to(dest_ref[...], (PAGE, TOKENS))
        along = jnp.sum(jnp.where(token // PAGE == page, dest, 0), axis=0, keepdims=True)
        earlier = jnp.where((dest == along) & (page < token // PAGE), 1, 0)
        rank = jnp.sum(earlier, axis=0, keepdims=True)
        row = along * (CAP * PAGE) + rank * PAGE + token[0:1] % PAGE
        pick = lax.broadcasted_iota(jnp.int32, (4 * CAP * PAGE, TOKENS), 0) == row
        outgoing[...] = dot(jnp.where(pick, 1.0, 0.0).astype(BF16), cache[...]).astype(BF16).reshape(4, CAP * PAGE, WIDTH)
        page_own.append(fetch(outgoing.at[group], suffix.at[group], 13))
        for slot, name in enumerate(("sib", "twin", "cross")):
            copy = swap(outgoing.at[near[name][0]], suffix.at[group], slot, name, page_send, page_recv)
            copy.start()
            page_copies.append(copy)

    def attend(n):
        start = 96 * n // 128 * 128
        skip = 96 * n - start
        wide = 128 if skip + 96 <= 128 else 256
        query = jnp.concatenate([heads[2 * n], heads[2 * n + 1]], axis=1)
        rows = [query]
        if skip:
            rows = [jnp.zeros((skip, 2 * TOKENS), BF16)] + rows
        if wide - skip - 96:
            rows = rows + [jnp.zeros((wide - skip - 96, 2 * TOKENS), BF16)]
        query = jnp.concatenate(rows, axis=0)
        window = slice(start, start + wide)
        scores = [dot(pages[0, z, :, :, :, window].reshape(256, wide), query) for z in range(4)]
        allowed = mask[...]
        allowed = jnp.concatenate([allowed, allowed], axis=1) > 0.5
        scores.append(jnp.where(allowed, dot(cache[:, window], query), NEGATIVE_FILLER))
        values = [pages[1, z, :, :, :, window].reshape(256, wide) for z in range(4)]
        values.append(cache[:, slice(HALF + start, HALF + start + wide)])
        top = scores[0].max(axis=0, keepdims=True)
        for part in scores[1:]:
            top = jnp.maximum(top, part.max(axis=0, keepdims=True))
        scale = HEAD_DIMENSION ** (-0.5) * 1.4426950408889634
        whole, summed = None, None
        for part, value in zip(scores, values):
            weight = jnp.exp2((part - top) * scale)
            mass = jnp.sum(weight, axis=0, keepdims=True)
            product = lax.dot_general(
                value, weight.astype(BF16), (((0,), (0,)), ((), ())), preferred_element_type=F32
            )
            whole = mass if whole is None else whole + mass
            summed = product if summed is None else summed + product
        out = summed[skip : skip + 96] / whole
        mixed[2 * n] = out[:, :TOKENS]
        mixed[2 * n + 1] = out[:, TOKENS:]

    def leave():
        out_load.wait()
        attended = mixed[...].reshape(WIDTH, TOKENS).T.astype(BF16)
        summed = (hidden[...].astype(F32) + dot(attended, w_out[...])).astype(BF16)
        middle[...] = summed
        tokens[0] = norm_rows(summed.astype(F32), gains[1:2]).astype(BF16)
        copy = swap(tokens.at[0], tokens.at[1], 0, "sib", swap_send, swap_recv)
        copy.start()
        swaps.append(copy)
        total[...] = jnp.zeros_like(total)

    def feed(z, high):
        if (z, high) == (0, 0):
            swaps[0].wait_recv()
        both = tokens[...].reshape(2 * TOKENS, WIDTH)
        low_half = lax.broadcasted_iota(jnp.int32, (2 * TOKENS, 128), 1) < 64
        active = []
        for pair in range(2):
            joined = jnp.concatenate([win[z, high, 2 * pair], win[z, high, 2 * pair + 1]], axis=1)
            product = dot(both, joined)
            one, two = product[:, :128], product[:, 128:]
            gate_part = jnp.where(low_half, one, pltpu.roll(two, 64, 1))
            up_part = jnp.where(low_half, pltpu.roll(one, 64, 1), two)
            active.append((gate_part / (1.0 + jnp.exp(-gate_part)) * up_part).astype(BF16))
        total[...] += dot(jnp.concatenate(active, axis=1), wdown[z, high].reshape(256, WIDTH))

    def finish():
        sent[...] = total[TOKENS:].astype(BF16)
        copy = swap(sent, received, 1, "sib", swap_send, swap_recv)
        copy.start()
        swaps.append(copy)
        mine = middle[...].astype(F32) + total[:TOKENS]
        copy.wait_recv()
        result[...] = (mine + received[...].astype(F32)).astype(BF16)

    work = [(prepare, 2000.0, ())]
    work += [(functools.partial(project, n), 1000.0, ()) for n in range(8)]
    work += [(send_pages, 2000.0, ())]
    work += [(functools.partial(attend, n), 2500.0, prefix_done) for n in range(8)]
    work += [(leave, 4000.0, ())]
    work += [(functools.partial(feed, z, high), 2500.0, covers(plan, z, high)) for high in range(2) for z in range(4)]
    work += [(finish, 3000.0, ())]

    copies, arrived = {}, set()

    def await_all(needs):
        for k in needs:
            if k not in arrived:
                copies[k].wait_recv()
                arrived.add(k)

    order, _, _ = plan.order(work)
    for kind, item in order:
        if kind == "work":
            await_all(item[2])
            item[0]()
            continue
        name, source, target, direction, after, _ = plan.copies[item]
        await_all(after)
        copies[item] = swap(place(name, source), place(name, target), item, direction, send, recv)
        copies[item].start()
    await_all(range(len(plan.copies)))
    for copy in copies.values():
        copy.wait_send()
    for copy in rivals + swaps:
        copy.wait_send()
    for copy in page_copies:
        copy.wait()
    page_own[0].wait()


def layer(*operands):
    count = len(gather_plan()[0].copies)
    vmem = pl.BlockSpec(memory_space=pltpu.VMEM)
    anywhere = pl.BlockSpec(memory_space=pl.ANY)
    dma = pltpu.SemaphoreType.DMA
    return pl.pallas_call(
        layer_kernel,
        out_shape=(
            jax.ShapeDtypeStruct((TOKENS, WIDTH), BF16),
            jax.ShapeDtypeStruct((4, CAP * PAGE, WIDTH), BF16),
        ),
        in_specs=[vmem] * 6 + [anywhere] * 5,
        out_specs=(vmem, anywhere),
        scratch_shapes=[
            pltpu.VMEM((2, WIDTH, 128), BF16),
            pltpu.VMEM((2, 32, HALF), BF16),
            pltpu.VMEM((3, 32, HALF), BF16),
            pltpu.VMEM((4, 2, 4, WIDTH, 128), BF16),
            pltpu.VMEM((4, 2, 4, 64, WIDTH), BF16),
            pltpu.VMEM((2, 4, 2, 4, 32, HALF), BF16),
            pltpu.VMEM((8, WIDTH, 384), BF16),
            pltpu.VMEM((WIDTH, WIDTH), BF16),
            pltpu.VMEM((TOKENS, WIDTH), BF16),
            pltpu.VMEM((QUERY_HEADS, HEAD_DIMENSION, TOKENS), BF16),
            pltpu.VMEM((QUERY_HEADS, HEAD_DIMENSION, TOKENS), F32),
            pltpu.VMEM((HEAD_DIMENSION, TOKENS), F32),
            pltpu.VMEM((TOKENS, TOKENS), F32),
            pltpu.VMEM((4, CAP * PAGE, WIDTH), BF16),
            pltpu.VMEM((2, TOKENS, WIDTH), BF16),
            pltpu.VMEM((TOKENS, WIDTH), BF16),
            pltpu.VMEM((TOKENS, WIDTH), BF16),
            pltpu.VMEM((2 * TOKENS, WIDTH), F32),
            pltpu.VMEM((TOKENS, WIDTH), BF16),
            pltpu.VMEM((TOKENS, WIDTH), BF16),
            dma((14,)), dma((3,)), dma((3,)), dma((count,)), dma((count,)), dma((2,)), dma((2,)), dma((3,)), dma((3,)),
        ],
        compiler_params=pltpu.CompilerParams(
            collective_id=0, has_side_effects=True, vmem_limit_bytes=67043328
        ),
    )(*operands)


def on_device(
    hidden_in,
    request_ids,
    norm_gains,
    query_key_value_weight,
    w_out,
    w_in,
    w_down,
    prefix_cache,
    prefix_owner,
    page_dest,
):
    hidden_out, suffix = layer(
        hidden_in, request_ids, norm_gains, prefix_owner.reshape(1, -1), page_dest, jnp.asarray(rope_table()),
        query_key_value_weight, w_out, w_in, w_down, prefix_cache,
    )
    return (hidden_out, suffix.reshape(1, 1, 4, CAP, PAGE, WIDTH))


def solution(mesh):
    return jax.shard_map(
        on_device,
        mesh=mesh,
        in_specs=(
            P(("group", "tensor"), None),
            P(("group", "tensor"), None),
            P(),
            P(),
            P(),
            P(None, None, "tensor"),
            P("tensor", None),
            P("group", "tensor", None),
            P(),
            P(("group", "tensor"), None),
        ),
        out_specs=(P(("group", "tensor"), None), P("group", "tensor", None, None, None, None)),
        check_vma=False,
    )
```
